32 devices in a mesh: tower: 4 (over y, x), member: 8 (over z, core).
Axes of the slice: x: 2, y: 2, z: 4, core: 2. Of those that a mesh axis runs over, the one named last changes fastest.
Arguments:
- bag_ids: int32 [8, 8, 4, 512], P('tower', 'member'), may hold values from 0 to 511
- touch_ids: int32 [8, 8, 128], P('tower', 'member'), may hold values from 0 to 511, as said below
- elapsed: int32 [8, 8, 128], P('tower', 'member'), may hold values from 0 to 39
- tables: float32 [8, 8, 512, 64], P('tower', 'member'), may hold values from -3 to 3
- accumulator: float32 [8, 8, 512], P('tower', 'member'), may hold values from 0.001 to 0.1
- first_weight: float32 [512, 8, 1024], P(None, 'tower'), may hold values from -0.25 to 0.25
- second_weight: float32 [1024, 8, 256], P(None, 'tower'), may hold values from -0.1875 to 0.1875
- lift_weight: float32 [2048, 128], replicated, may hold values from -0.5 to 0.5
- press_weight: float32 [2048, 128], replicated, may hold values from -0.125 to 0.125
- head_weight: float32 [2048], replicated, may hold values from -0.125 to 0.125
- labels: int32 [8, 64], P('member'), may hold values 0 or 1
Outputs:
- new_tables: float32 [8, 8, 512, 64], P('tower', 'member')
- new_accumulator: float32 [8, 8, 512], P('tower', 'member')
- grad_first: float32 [512, 8, 1024], P('member', 'tower')
- grad_second: float32 [1024, 8, 256], P('member', 'tower')
- grad_lift: float32 [2048, 128], P(('tower', 'member'))
- grad_press: float32 [2048, 128], P(('tower', 'member'))
- logits: float32 [8, 64], P('member', 'tower')
The draws below stay inside these ranges and needn't reach their ends.
Inputs may be any that keep to these rules, and one draw needn't show every extreme that they name: `touch_ids`: distinct within each table.
All inputs are finite; a program needn't handle non-finite values. No bound on the sum of `labels` on one device may be relied on, other than what follows from the above.
Results may differ from the reference program's by a relative error of at most 0.0003.
Values sent between devices are 32-bit elements; how exact they have to be, the bound alone decides.
A program may use at most 128 MiB of HBM per device.

```python
import math
import jax
import jax.numpy as jnp
import numpy as np
from jax import lax

W = 64
HID = 1024
TOUT = 256
RANK = 128
BAG = 4
ROWS = 512
TOUCH = 128
TOWERS = 8
TTAB = 8
FIN = 512
CROSS = 2048
SAMP = 64
SAMPLES = 512
N_MEMBER = 8


def draw_touch_ids(key, part):
    keys = jax.random.split(jax.random.fold_in(key, 7), TOWERS * TTAB)

    def one_table(table_key):
        perm_key, shift_key = jax.random.split(table_key)
        others = (jax.random.permutation(perm_key, ROWS - 2)[:TOUCH - 2] + 1).astype(jnp.int32)
        listed = jnp.concatenate([jnp.full((1,), ROWS - 1, jnp.int32), jnp.zeros((1,), jnp.int32), others])
        shift = jax.random.randint(shift_key, (), 0, TOUCH)
        return jnp.roll(listed, shift)
    return jax.vmap(one_table)(keys).reshape(TOWERS, TTAB, TOUCH).astype(jnp.int32)


def place_ends(values, own_key, least, top_value):
    spot = [jax.random.randint(jax.random.fold_in(own_key, axis), (), 0, length) for axis, length in enumerate(values.shape)]
    longest = values.shape.index(max(values.shape))
    neighbour = spot[:longest] + [(spot[longest] + 1) % values.shape[longest]] + spot[longest + 1:]
    return values.at[tuple(spot)].set(least).at[tuple(neighbour)].set(top_value)


def level_of(key, extent, pieces, smallest, top_value):
    level = 1.0
    for dim, blocks in pieces:
        draws = jax.random.uniform(jax.random.fold_in(jax.random.fold_in(key, 6), dim), (blocks,), jnp.float32, smallest / len(pieces), top_value / len(pieces))
        level = level * jnp.repeat(jnp.exp(draws), extent[dim] // blocks).reshape((-1,) + (1,) * (len(extent) - 1 - dim))
    return level


def cumulative_ranks(count, slope):
    loads = [(1 << 20) // math.isqrt(standing ** slope) + 1 for standing in range(1, count + 1)]
    width = 1 + sum(loads) // (1 << 30)
    return np.cumsum(np.array([max(1, weight // width) for weight in loads]))


def ranked_ids(stream_key, shape, number_of, lean):
    table = cumulative_ranks(number_of, lean)
    pick = jax.random.randint(jax.random.fold_in(stream_key, 1), shape, 0, int(table[number_of - 1]))
    grade = jnp.searchsorted(jnp.asarray(table, jnp.int32), pick, side="right")
    return jax.random.permutation(jax.random.fold_in(stream_key, 2), number_of)[grade].astype(jnp.int32)


def normal_values(key, dims, deviation, most, cuts=(), kind=jnp.bfloat16):
    array = jax.random.normal(key, dims, jnp.float32) * deviation
    if len(cuts) > 0:
        array = level_of(key, dims, cuts, -0.22, 0.18) * array
    return jnp.clip(array, min=-most, max=most).astype(kind)


def setup_inputs(seed: int = 0) -> dict:
    key_of = jax.random.split(jax.random.key(seed), 12)
    bag_ids = place_ends(ranked_ids(key_of[0], (TOWERS, TTAB, BAG, SAMPLES), ROWS, 2), jax.random.fold_in(key_of[0], 3), 0, ROWS - 1).astype(jnp.int32)
    touch_ids = draw_touch_ids(jax.random.fold_in(key_of[11], 71), 0)
    elapsed = place_ends(jax.random.randint(key_of[2], (TOWERS, TTAB, TOUCH), 0, 40), jax.random.fold_in(key_of[2], 1), 0, 39).astype(jnp.int32)
    tables = normal_values(key_of[3], (TOWERS, TTAB, ROWS, W), 0.5, 3.0, ((0, 4), (1, 8)), jnp.float32)
    accumulator = jnp.clip(jnp.exp(math.log(0.1) - 4.6051702 * jax.random.uniform(key_of[4], (TOWERS, TTAB, ROWS), jnp.float32) ** level_of(key_of[4], (TOWERS, TTAB, ROWS), ((0, 4), (1, 8)), -0.2, 0.2)), 0.001, 0.1)
    first_weight = normal_values(key_of[5], (FIN, TOWERS, HID), FIN ** -0.5, 0.25, ((1, 4),), jnp.float32)
    second_weight = normal_values(key_of[6], (HID, TOWERS, TOUT), HID ** -0.5, 0.1875, ((1, 4),), jnp.float32)
    lift_weight = normal_values(key_of[7], (CROSS, RANK), RANK ** -0.5, 0.5, (), jnp.float32)
    press_weight = normal_values(key_of[8], (CROSS, RANK), CROSS ** -0.5, 0.125, (), jnp.float32)
    head_weight = normal_values(key_of[9], (CROSS,), CROSS ** -0.5, 0.125, (), jnp.float32)
    labels = place_ends((jax.random.randint(key_of[10], (N_MEMBER, SAMP), 0, 2) < 1).astype(jnp.int32), jax.random.fold_in(key_of[10], 1), 0, 1)
    return dict(bag_ids=bag_ids, touch_ids=touch_ids, elapsed=elapsed, tables=tables, accumulator=accumulator, first_weight=first_weight, second_weight=second_weight, lift_weight=lift_weight, press_weight=press_weight, head_weight=head_weight, labels=labels)


PRECISE = lax.Precision.HIGHEST
DECAY_RATE = 0.98
LEARN_RATE = 1.0
EPSILON = 1e-08

def decay_factors(touch_ids, elapsed, table_rows):
    rates = jnp.exp(elapsed.astype(jnp.float32) * math.log(DECAY_RATE))
    matches = touch_ids[..., None] == jnp.arange(table_rows, dtype=jnp.int32)
    hits = lax.optimization_barrier(jnp.sum(matches.astype(jnp.float32), axis=-2))
    chosen = lax.optimization_barrier(jnp.sum(jnp.where(matches, rates[..., None], jnp.float32(0.0)), axis=-2))
    return jnp.where(hits > 0.0, chosen, jnp.float32(1.0))

def pool_table(decayed_table, bag_table):
    return lax.optimization_barrier(jnp.sum(decayed_table[bag_table], axis=0))

def reference(bag_ids, touch_ids, elapsed, tables, accumulator, first_weight, second_weight, lift_weight, press_weight, head_weight, labels):
    factors = lax.map(lambda inputs: decay_factors(inputs[0], inputs[1], ROWS), (touch_ids, elapsed))
    decayed = tables * factors[..., None]

    def forward(decayed_tables, weight_one, weight_two, lift, press):
        pooled = lax.map(lambda inputs: jax.vmap(pool_table)(inputs[0], inputs[1]), (decayed_tables, bag_ids))
        features = jnp.transpose(pooled, (2, 0, 1, 3)).reshape(SAMPLES, TOWERS, FIN)
        hidden = jnp.einsum('sti,ith->sth', features, weight_one, precision=PRECISE)
        tower_out = jnp.einsum('sth,hto->sto', jax.nn.silu(hidden), weight_two, precision=PRECISE)
        start_rows = tower_out.reshape(SAMPLES, CROSS)
        projected = jnp.dot(start_rows, press, precision=PRECISE)
        scaling = jnp.dot(projected, lift.T, precision=PRECISE)
        crossed = start_rows * scaling + start_rows
        return jnp.dot(crossed, head_weight, precision=PRECISE)
    logit_values, pullback = jax.vjp(forward, decayed, first_weight, second_weight, lift_weight, press_weight)
    errors = jax.nn.sigmoid(logit_values) - labels.reshape(SAMPLES).astype(jnp.float32)
    grad_tables, grad_one, grad_two, grad_lift, grad_press = pullback(errors)
    mean_square = lax.optimization_barrier(jnp.mean(grad_tables * grad_tables, axis=-1))
    new_accumulator = accumulator + mean_square
    new_tables = decayed - LEARN_RATE * grad_tables / (jnp.sqrt(new_accumulator)[..., None] + EPSILON)
    return (new_tables, new_accumulator, grad_one, grad_two, grad_lift, grad_press, logit_values.reshape(N_MEMBER, SAMP))
```

```python
import functools
import math

import jax
import jax.numpy as jnp
from jax import lax
from jax.experimental import pallas as pl
from jax.experimental.pallas import tpu as pltpu
from jax.sharding import PartitionSpec as P

MESH = pl.DeviceIdType.MESH
DECAY_RATE = 0.98
LEARN_RATE = 1.0
EPSILON = 1e-08
F32 = jnp.float32
BF16 = jnp.bfloat16
NN = (((1,), (0,)), ((), ()))
NT = (((1,), (1,)), ((), ()))


def split(x):
    hi = x.astype(BF16)
    return hi, (x - hi.astype(F32)).astype(BF16)


def dot1(a, b, dims=NN):
    return lax.dot_general(a, b, dims, preferred_element_type=F32)


def dot3(a, b, dims=NN):
    (ah, al), (bh, bl) = a, b
    return dot1(ah, bh, dims) + (dot1(ah, bl, dims) + dot1(al, bh, dims))


def sigmoid(x):
    return 1.0 / (1.0 + jnp.exp(-x))


def kernel(
    dims,
    bag_ref,
    touch_ref,
    elapsed_ref,
    tables_ref,
    acc_ref,
    first_hbm,
    second_hbm,
    lift_hbm,
    press_hbm,
    head_ref,
    label_ref,
    new_tables_ref,
    new_acc_ref,
    grad_first_ref,
    grad_second_ref,
    grad_lift_ref,
    grad_press_ref,
    logits_ref,
    w1h,
    w1l,
    w2f,
    w2h,
    w2l,
    lift,
    press,
    decayed,
    cols,
    feats,
    hidden,
    act,
    stats,
    rs_buf,
    gath,
    gl,
    gp,
    gsec,
    gt,
    load_sem,
    ag_send,
    ag_recv,
    rs_send,
    rs_recv,
    gm_send,
    gm_recv,
    gt_send,
    gt_recv,
):
    n, nt = dims
    me = lax.axis_index("member")
    tpos = lax.axis_index("tower")
    towers, bags, total = bag_ref.shape
    rows, width = tables_ref.shape[1:]
    hid, outs = w2f.shape[1:]
    fin = w1h.shape[1]
    rank = lift.shape[1]
    flat = towers * outs
    own = total // n
    piece = own // nt
    chunk = min(256, total)
    chips = n // 2
    chip, core = me // 2, lax.rem(me, 2)

    loads = []
    for t in range(towers):
        loads.append(pltpu.make_async_copy(first_hbm.at[t], hidden.at[t, :fin], load_sem.at[len(loads)]))
        loads.append(pltpu.make_async_copy(second_hbm.at[t], w2f.at[t], load_sem.at[len(loads)]))
    loads.append(
        pltpu.make_async_copy(lift_hbm.at[pl.ds(tpos * flat, flat)], lift, load_sem.at[len(loads)])
    )
    loads.append(
        pltpu.make_async_copy(press_hbm.at[pl.ds(tpos * flat, flat)], press, load_sem.at[len(loads)])
    )
    for load in loads:
        load.start()

    barrier = pltpu.get_barrier_semaphore()
    for d in range(1, n):
        pl.semaphore_signal(
            barrier, inc=1, device_id={"member": lax.rem(me + d, n)}, device_id_type=MESH
        )
    for d in range(1, nt):
        pl.semaphore_signal(
            barrier, inc=1, device_id={"tower": lax.rem(tpos + d, nt)}, device_id_type=MESH
        )

    stack = [bag_ref[t].astype(F32) for t in range(towers)]
    used = towers * bags
    stack.append(jnp.zeros((128 - used, total), F32))
    cols[...] = jnp.concatenate(stack, axis=0).T

    for t in range(towers):
        rates = jnp.exp(elapsed_ref[t : t + 1, :].astype(F32) * math.log(DECAY_RATE))
        ids = touch_ref[t : t + 1, :]
        place = lax.broadcasted_iota(jnp.int32, (rows, ids.shape[1]), 0)
        chosen = jnp.sum(jnp.where(place == ids, rates, 0.0), axis=1, keepdims=True)
        decayed[t] = tables_ref[t] * jnp.where(chosen > 0.0, chosen, 1.0)
    pairs = [jnp.concatenate(split(decayed[t]), axis=1) for t in range(towers)]
    for c in range(total // chunk):
        span = pl.ds(c * chunk, chunk)
        place = lax.broadcasted_iota(jnp.int32, (chunk, rows), 1).astype(F32)
        pooled = []
        for t in range(towers):
            counts = jnp.zeros((chunk, rows), F32)
            for b in range(bags):
                k = t * bags + b
                counts = counts + jnp.where(place == cols[span, k : k + 1], 1.0, 0.0)
            both = dot1(counts.astype(BF16), pairs[t])
            pooled.append(both[:, :width] + both[:, width:])
        feats[me, span, :] = jnp.concatenate(pooled, axis=1)

    pl.semaphore_wait(barrier, n - 1 + nt - 1)

    def block_copy(block, lane, target):
        return pltpu.make_async_remote_copy(
            src_ref=feats.at[block],
            dst_ref=feats.at[block],
            send_sem=ag_send.at[lane, block],
            recv_sem=ag_recv.at[block],
            device_id={"member": target},
            device_id_type=MESH,
        )

    def pass_on(block, right, left):
        if right:

            @pl.when(chip + 1 < chips)
            def _():
                block_copy(block, 0, me + 2).start()

        if left:

            @pl.when(chip > 0)
            def _():
                block_copy(block, 1, me - 2).start()

        block_copy(block, 2, me + 1 - 2 * core).start()

    def sent(block, right, left):
        if right:

            @pl.when(chip + 1 < chips)
            def _():
                block_copy(block, 0, me + 2).wait_send()

        if left:

            @pl.when(chip > 0)
            def _():
                block_copy(block, 1, me - 2).wait_send()

        block_copy(block, 2, me + 1 - 2 * core).wait_send()

    pass_on(me, True, True)

    for load in loads:
        load.wait()
    for t in range(towers):

        @pl.loop(0, fin // 64)
        def _(i):
            span = pl.ds(pl.multiple_of(i * 64, 64), 64)
            w1h[t, span, :], w1l[t, span, :] = split(hidden[t, span, :])

        @pl.loop(0, hid // 128)
        def _(i):
            span = pl.ds(pl.multiple_of(i * 128, 128), 128)
            w2h[t, span, :], w2l[t, span, :] = split(w2f[t, span, :])

    for d in range(1, chips):

        @pl.when(chip >= d)
        def _():
            block = me - 2 * d
            block_copy(block, 0, me).wait_recv()
            pass_on(block, True, False)

        @pl.when(chip + d < chips)
        def _():
            block = me + 2 * d
            block_copy(block, 0, me).wait_recv()
            pass_on(block, False, True)

    for c in range(chips):
        block_copy(2 * c + 1 - core, 0, me).wait_recv()

    sent(me, True, True)
    for d in range(1, chips):

        @pl.when(chip >= d)
        def _():
            sent(me - 2 * d, True, False)

        @pl.when(chip + d < chips)
        def _():
            sent(me + 2 * d, False, True)

    def features_of(t, span):
        return jnp.concatenate(
            [feats[j, span, t * width : (t + 1) * width] for j in range(n)], axis=1
        )

    head = head_ref[:, pl.ds(pl.multiple_of(tpos * flat, flat), flat)]
    lift_pair = split(lift[...])
    press_pair = split(press[...])

    mine = pl.ds(pl.multiple_of(me * own, own), own)
    flat_out = []
    for t in range(towers):
        h = dot3(split(features_of(t, mine)), (w1h[t], w1l[t]))
        flat_out.append(dot3(split(h * sigmoid(h)), (w2h[t], w2l[t])))
    flat_out = jnp.concatenate(flat_out, axis=1)
    weighted = flat_out * head
    stats[:, :rank] = dot3(split(flat_out), press_pair)
    stats[:, rank : 2 * rank] = dot3(split(weighted), lift_pair)
    stats[:, 2 * rank :] = jnp.broadcast_to(
        jnp.sum(weighted, axis=1, keepdims=True), (own, rank)
    )

    def tower_copy(d, reverse=False):
        other = lax.rem(tpos + d, nt)
        return pltpu.make_async_remote_copy(
            src_ref=stats.at[pl.ds(pl.multiple_of(other * piece, piece), piece)],
            dst_ref=rs_buf.at[tpos],
            send_sem=rs_send.at[d],
            recv_sem=rs_recv.at[d],
            device_id={"tower": other},
            device_id_type=MESH,
        )

    for d in range(1, nt):
        tower_copy(d).start()

    @pl.loop(0, total // chunk)
    def _(c):
        span = pl.ds(pl.multiple_of(c * chunk, chunk), chunk)
        for t in range(towers):
            hidden[t, span, :] = dot3(split(features_of(t, span)), (w1h[t], w1l[t]))

    for d in range(1, nt):
        tower_copy(d).wait_recv()
    summed = stats[pl.ds(pl.multiple_of(tpos * piece, piece), piece), :]
    for d in range(1, nt):
        summed = summed + rs_buf[lax.rem(tpos + d, nt)]
    logit = (
        jnp.sum(summed[:, :rank] * summed[:, rank : 2 * rank], axis=1, keepdims=True)
        + summed[:, 2 * rank :]
    )
    logits_ref[...] = logit
    error = sigmoid(logit) - label_ref[...]
    gath[me, tpos, :, :rank] = error * summed[:, :rank]
    gath[me, tpos, :, rank : 2 * rank] = error * summed[:, rank : 2 * rank]
    gath[me, tpos, :, 2 * rank :] = error
    for d in range(1, nt):
        tower_copy(d).wait_send()

    def member_copy(d):
        return pltpu.make_async_remote_copy(
            src_ref=gath.at[me, tpos],
            dst_ref=gath.at[me, tpos],
            send_sem=gm_send.at[d],
            recv_sem=gm_recv.at[d],
            device_id={"member": lax.rem(me + d, n)},
            device_id_type=MESH,
        )

    for d in range(1, n):
        member_copy(d).start()
    for d in range(1, n):
        member_copy(d).wait_recv()

    def column_copy(d):
        return pltpu.make_async_remote_copy(
            src_ref=gath.at[:, tpos],
            dst_ref=gath.at[:, tpos],
            send_sem=gt_send.at[d],
            recv_sem=gt_recv.at[d],
            device_id={"tower": lax.rem(tpos + d, nt)},
            device_id_type=MESH,
        )

    for d in range(1, nt):
        column_copy(d).start()
    for d in range(1, nt):
        column_copy(d).wait_recv()
    for d in range(1, n):
        member_copy(d).wait_send()
    for d in range(1, nt):
        column_copy(d).wait_send()

    block_hid = hid // n
    window = max(block_hid, 128)
    start = pl.multiple_of((me * block_hid) // 128 * 128, 128)
    grad_first_ref[...] = jnp.zeros_like(grad_first_ref)
    gsec[...] = jnp.zeros_like(gsec)
    gl[...] = jnp.zeros_like(gl)
    gp[...] = jnp.zeros_like(gp)
    gt[...] = jnp.zeros_like(gt)
    own_rows = pl.ds(pl.multiple_of(me * width, width), width)
    members_here = chunk // own

    for t in range(towers):

        @pl.loop(0, total // chunk)
        def _(c):
            span = pl.ds(pl.multiple_of(c * chunk, chunk), chunk)
            block = gath[pl.ds(c * members_here, members_here)].reshape(chunk, 3 * rank)
            ep = split(block[:, :rank])
            eg = split(block[:, rank : 2 * rank])
            part = slice(t * outs, (t + 1) * outs)
            head_t = head[:, part]
            lift_t = tuple(x[part] for x in lift_pair)
            press_t = tuple(x[part] for x in press_pair)
            w2 = (w2h[t], w2l[t])
            error_all = block[:, 2 * rank : 2 * rank + 1]
            grad_out = head_t * (error_all + dot3(ep, lift_t, NT)) + dot3(eg, press_t, NT)
            h = hidden[t, span, :]
            sig = sigmoid(h)
            a = h * sig
            act[...] = a
            tower_out = dot3(split(a), w2)
            gl[part] += dot3(split((tower_out * head_t).T), ep)
            gp[part] += dot3(split(tower_out.T), eg)
            go = split(grad_out)
            gsec[t] += dot3(split(act[:, pl.ds(start, window)].T), go)
            grad_hidden = split(dot3(go, w2, NT) * (sig * (1.0 + h * (1.0 - sig))))
            pooled = feats[me, span, :].T[t * width : (t + 1) * width]
            grad_first_ref[t] += dot3(split(pooled), grad_hidden)
            grad_pooled = dot3(grad_hidden, (w1h[t, own_rows, :], w1l[t, own_rows, :]), NT)
            counts = jnp.zeros((rows, chunk), F32)
            place = lax.broadcasted_iota(jnp.int32, (rows, chunk), 0)
            for b in range(bags):
                counts = counts + jnp.where(place == bag_ref[t, b : b + 1, span], 1.0, 0.0)
            both = dot1(counts.astype(BF16), jnp.concatenate(split(grad_pooled), axis=1))
            gt[t] += both[:, :width] + both[:, width:]

        shift = pl.multiple_of(me * block_hid - start, min(block_hid, 128))
        grad_second_ref[t] = gsec[t, pl.ds(shift, block_hid), :]

    own_flat = pl.ds(pl.multiple_of(me * (flat // n), flat // n), flat // n)
    grad_lift_ref[...] = gl[own_flat]
    grad_press_ref[...] = gp[own_flat]
    squares = []
    for t in range(towers):
        g = gt[t]
        squares.append(jnp.mean(g * g, axis=1, keepdims=True))
    wide = jnp.concatenate(squares + [jnp.zeros((rows, 128 - towers), F32)], axis=1).T
    new_acc_ref[...] = acc_ref[...] + wide[:towers]
    back = jnp.concatenate([acc_ref[...], jnp.zeros((128 - towers, rows), F32)], axis=0).T
    for t in range(towers):
        value = back[:, t : t + 1] + squares[t]
        new_tables_ref[t] = decayed[t] - LEARN_RATE * gt[t] / (jnp.sqrt(value) + EPSILON)


def per_device(n, nt, *args):
    bag_ids, touch_ids, elapsed, tables, accumulator, first, second, lift, press, head, labels = args
    towers, _, bags, total = bag_ids.shape
    rows, width = tables.shape[2:]
    fin, _, hid = first.shape
    outs = second.shape[2]
    rank = lift.shape[1]
    flat = towers * outs
    own = total // n
    piece = own // nt
    window = max(hid // n, 128)
    tpos = lax.axis_index("tower")
    label = lax.dynamic_slice_in_dim(labels[0], tpos * piece, piece, 0).astype(F32)
    label = jnp.broadcast_to(label[:, None], (piece, rank))
    vmem = pl.BlockSpec(memory_space=pltpu.VMEM)
    anys = pl.BlockSpec(memory_space=pl.ANY)
    chunk = min(256, total)
    sem = pltpu.SemaphoreType.DMA
    out = pl.pallas_call(
        functools.partial(kernel, (n, nt)),
        out_shape=(
            jax.ShapeDtypeStruct((towers, rows, width), F32),
            jax.ShapeDtypeStruct((towers, rows), F32),
            jax.ShapeDtypeStruct((towers, fin // n, hid), F32),
            jax.ShapeDtypeStruct((towers, hid // n, outs), F32),
            jax.ShapeDtypeStruct((flat // n, rank), F32),
            jax.ShapeDtypeStruct((flat // n, rank), F32),
            jax.ShapeDtypeStruct((piece, rank), F32),
        ),
        in_specs=[vmem] * 5 + [anys] * 4 + [vmem] * 2,
        out_specs=[vmem] * 7,
        scratch_shapes=[
            pltpu.VMEM((towers, fin, hid), BF16),
            pltpu.VMEM((towers, fin, hid), BF16),
            pltpu.VMEM((towers, hid, outs), F32),
            pltpu.VMEM((towers, hid, outs), BF16),
            pltpu.VMEM((towers, hid, outs), BF16),
            pltpu.VMEM((flat, rank), F32),
            pltpu.VMEM((flat, rank), F32),
            pltpu.VMEM((towers, rows, width), F32),
            pltpu.VMEM((total, 128), F32),
            pltpu.VMEM((n, total, towers * width), F32),
            pltpu.VMEM((towers, max(total, fin), hid), F32),
            pltpu.VMEM((chunk, hid), F32),
            pltpu.VMEM((own, 3 * rank), F32),
            pltpu.VMEM((nt, piece, 3 * rank), F32),
            pltpu.VMEM((n, nt, piece, 3 * rank), F32),
            pltpu.VMEM((flat, rank), F32),
            pltpu.VMEM((flat, rank), F32),
            pltpu.VMEM((towers, window, outs), F32),
            pltpu.VMEM((towers, rows, width), F32),
            sem((2 * towers + 2,)),
            sem((3, n)),
            sem((n,)),
            sem((nt,)),
            sem((nt,)),
            sem((n,)),
            sem((n,)),
            sem((nt,)),
            sem((nt,)),
        ],
        compiler_params=pltpu.CompilerParams(
            collective_id=0, has_side_effects=True, vmem_limit_bytes=67043328
        ),
    )(
        bag_ids[:, 0],
        touch_ids[:, 0],
        elapsed[:, 0],
        tables[:, 0],
        accumulator[:, 0],
        jnp.transpose(first, (1, 0, 2)),
        jnp.transpose(second, (1, 0, 2)),
        lift,
        press,
        head[None, :],
        label,
    )
    new_tables, new_acc, grad_first, grad_second, grad_lift, grad_press, logits = out
    return (
        new_tables[:, None],
        new_acc[:, None],
        jnp.transpose(grad_first, (1, 0, 2)),
        jnp.transpose(grad_second, (1, 0, 2)),
        grad_lift,
        grad_press,
        logits[:, 0][None, :],
    )


def solution(mesh):
    placed = (
        P("tower", "member", None, None),
        P("tower", "member", None),
        P("tower", "member", None),
        P("tower", "member", None, None),
        P("tower", "member", None),
        P(None, "tower", None),
        P(None, "tower", None),
        P(),
        P(),
        P(),
        P("member", None),
    )
    return jax.shard_map(
        functools.partial(per_device, mesh.shape["member"], mesh.shape["tower"]),
        mesh=mesh,
        in_specs=placed,
        out_specs=(
            P("tower", "member", None, None),
            P("tower", "member", None),
            P("member", "tower", None),
            P("member", "tower", None),
            P(("tower", "member"), None),
            P(("tower", "member"), None),
            P("member", "tower"),
        ),
        check_vma=False,
    )
```

```python
import functools
import math

import jax
import jax.numpy as jnp
from jax import lax
from jax.experimental import pallas as pl
from jax.experimental.pallas import tpu as pltpu
from jax.sharding import PartitionSpec as P

MESH = pl.DeviceIdType.MESH
DECAY_RATE = 0.98
LEARN_RATE = 1.0
EPSILON = 1e-08
F32 = jnp.float32
BF16 = jnp.bfloat16
NN = (((1,), (0,)), ((), ()))
NT = (((1,), (1,)), ((), ()))


def split(x):
    hi = x.astype(BF16)
    return hi, (x - hi.astype(F32)).astype(BF16)


def dot1(a, b, dims=NN):
    return lax.dot_general(a, b, dims, preferred_element_type=F32)


def dot3(a, b, dims=NN):
    (ah, al), (bh, bl) = a, b
    return dot1(ah, bh, dims) + (dot1(ah, bl, dims) + dot1(al, bh, dims))


def sigmoid(x):
    return 1.0 / (1.0 + jnp.exp(-x))


def gather_kernel(
    dims,
    bag_ref,
    touch_ref,
    elapsed_ref,
    tables_ref,
    first_hbm,
    second_hbm,
    lift_hbm,
    press_hbm,
    head_ref,
    label_ref,
    logits_ref,
    decayed_ref,
    pooled_out,
    hidden_out,
    gath_out,
    counts_out,
    w2h_out,
    w2l_out,
    w1h,
    w1l,
    w2f,
    w2h,
    w2l,
    lift,
    press,
    cols,
    counts_ref,
    feats,
    hidden,
    stats,
    rs_buf,
    gath,
    load_sem,
    store_sem,
    hidden_sem,
    ag_send,
    ag_recv,
    rs_send,
    rs_recv,
    gm_send,
    gm_recv,
    gt_send,
    gt_recv,
):
    n, nt = dims
    me = lax.axis_index("member")
    tpos = lax.axis_index("tower")
    towers, bags, total = bag_ref.shape
    width, rows = tables_ref.shape[1:]
    touches = touch_ref.shape[2]
    hid, outs = w2h.shape[1:]
    fin = w1h.shape[1]
    rank = lift.shape[1]
    flat = towers * outs
    own = total // n
    piece = own // nt
    chunk = min(256, total)
    chips = n // 2
    chip, core = me // 2, lax.rem(me, 2)

    loads = []

    def load(source, target):
        loads.append(pltpu.make_async_copy(source, target, load_sem.at[len(loads)]))
        loads[-1].start()

    for t in range(towers):
        load(first_hbm.at[:, t, :], hidden.at[t, :fin])
        load(second_hbm.at[:, t, :], w2f.at[t])
    load(lift_hbm.at[pl.ds(tpos * flat, flat)], lift)
    load(press_hbm.at[pl.ds(tpos * flat, flat)], press)

    barrier = pltpu.get_barrier_semaphore()
    for d in range(1, n):
        pl.semaphore_signal(
            barrier, inc=1, device_id={"member": lax.rem(me + d, n)}, device_id_type=MESH
        )
    for d in range(1, nt):
        pl.semaphore_signal(
            barrier, inc=1, device_id={"tower": lax.rem(tpos + d, nt)}, device_id_type=MESH
        )

    stack = [bag_ref[t].astype(F32) for t in range(towers)]
    stack.append(jnp.zeros((128 - towers * bags, total), F32))
    cols[...] = jnp.concatenate(stack, axis=0).T
    stack = []
    for t in range(towers):
        stack.append(touch_ref[t].astype(F32))
        stack.append(jnp.exp(elapsed_ref[t].astype(F32) * math.log(DECAY_RATE)))
    stack.append(jnp.zeros((128 - 2 * towers, touches), F32))
    owed = jnp.concatenate(stack, axis=0).T
    pairs = []
    place = lax.broadcasted_iota(jnp.int32, (touches, rows), 1).astype(F32)
    for t in range(towers):
        ids, rates = owed[:, 2 * t : 2 * t + 1], owed[:, 2 * t + 1 : 2 * t + 2]
        chosen = jnp.sum(jnp.where(place == ids, rates, 0.0), axis=0, keepdims=True)
        decayed = tables_ref[t] * jnp.where(chosen > 0.0, chosen, 1.0)
        decayed_ref[t] = decayed
        pairs.append(jnp.concatenate(split(decayed), axis=0))
    for c in range(total // chunk):
        span = pl.ds(c * chunk, chunk)
        place = lax.broadcasted_iota(jnp.int32, (chunk, rows), 1).astype(F32)
        pooled = []
        for t in range(towers):
            counts = jnp.zeros((chunk, rows), F32)
            for b in range(bags):
                k = t * bags + b
                counts = counts + jnp.where(place == cols[span, k : k + 1], 1.0, 0.0)
            counts = counts.astype(BF16)
            counts_ref[t, span, :] = counts
            both = dot1(counts, pairs[t], NT)
            pooled.append(both[:, :width] + both[:, width:])
        feats[me, span, :] = jnp.concatenate(pooled, axis=1)

    pl.semaphore_wait(barrier, n - 1 + nt - 1)

    def block_copy(block, lane, target):
        return pltpu.make_async_remote_copy(
            src_ref=feats.at[block],
            dst_ref=feats.at[block],
            send_sem=ag_send.at[lane, block],
            recv_sem=ag_recv.at[block],
            device_id={"member": target},
            device_id_type=MESH,
        )

    def pass_on(block, right, left):
        if right:

            @pl.when(chip + 1 < chips)
            def _():
                block_copy(block, 0, me + 2).start()

        if left:

            @pl.when(chip > 0)
            def _():
                block_copy(block, 1, me - 2).start()

        block_copy(block, 2, me + 1 - 2 * core).start()

    def sent(block, right, left):
        if right:

            @pl.when(chip + 1 < chips)
            def _():
                block_copy(block, 0, me + 2).wait_send()

        if left:

            @pl.when(chip > 0)
            def _():
                block_copy(block, 1, me - 2).wait_send()

        block_copy(block, 2, me + 1 - 2 * core).wait_send()

    pass_on(me, True, True)

    stores = []

    def store(source, target):
        stores.append(pltpu.make_async_copy(source, target, store_sem.at[len(stores)]))
        stores[-1].start()

    store(counts_ref, counts_out)

    for copy in loads:
        copy.wait()
    for t in range(towers):

        @pl.loop(0, fin // 64)
        def _(i):
            span = pl.ds(pl.multiple_of(i * 64, 64), 64)
            w1h[t, span, :], w1l[t, span, :] = split(hidden[t, span, :])

        @pl.loop(0, hid // 128)
        def _(i):
            span = pl.ds(pl.multiple_of(i * 128, 128), 128)
            w2h[t, span, :], w2l[t, span, :] = split(w2f[t, span, :])

    store(w2h, w2h_out)
    store(w2l, w2l_out)
    store(feats.at[me], pooled_out)

    for d in range(1, chips):

        @pl.when(chip >= d)
        def _():
            block = me - 2 * d
            block_copy(block, 0, me).wait_recv()
            pass_on(block, True, False)

        @pl.when(chip + d < chips)
        def _():
            block = me + 2 * d
            block_copy(block, 0, me).wait_recv()
            pass_on(block, False, True)

    for c in range(chips):
        block_copy(2 * c + 1 - core, 0, me).wait_recv()

    def features_of(t, span):
        return jnp.concatenate(
            [feats[j, span, t * width : (t + 1) * width] for j in range(n)], axis=1
        )

    head = head_ref[:, pl.ds(pl.multiple_of(tpos * flat, flat), flat)]

    mine = pl.ds(pl.multiple_of(me * own, own), own)
    flat_out = []
    for t in range(towers):
        h = dot3(split(features_of(t, mine)), (w1h[t], w1l[t]))
        flat_out.append(dot3(split(h * sigmoid(h)), (w2h[t], w2l[t])))
    flat_out = jnp.concatenate(flat_out, axis=1)
    weighted = flat_out * head
    stats[:, :rank] = dot3(split(flat_out), split(press[...]))
    stats[:, rank : 2 * rank] = dot3(split(weighted), split(lift[...]))
    stats[:, 2 * rank :] = jnp.broadcast_to(
        jnp.sum(weighted, axis=1, keepdims=True), (own, rank)
    )

    def tower_copy(d):
        other = lax.rem(tpos + d, nt)
        return pltpu.make_async_remote_copy(
            src_ref=stats.at[pl.ds(pl.multiple_of(other * piece, piece), piece)],
            dst_ref=rs_buf.at[tpos],
            send_sem=rs_send.at[d],
            recv_sem=rs_recv.at[d],
            device_id={"tower": other},
            device_id_type=MESH,
        )

    for d in range(1, nt):
        tower_copy(d).start()

    def hidden_copy(t, c):
        span = pl.ds(pl.multiple_of(c * chunk, chunk), chunk)
        return pltpu.make_async_copy(
            hidden.at[t, span], hidden_out.at[t, span], hidden_sem.at[t, c]
        )

    def hidden_chunk(c):
        span = pl.ds(pl.multiple_of(c * chunk, chunk), chunk)
        for t in range(towers):
            hidden[t, span, :] = dot3(split(features_of(t, span)), (w1h[t], w1l[t]))
            hidden_copy(t, c).start()

    pl.loop(0, total // chunk)(hidden_chunk)

    for d in range(1, nt):
        tower_copy(d).wait_recv()
    summed = stats[pl.ds(pl.multiple_of(tpos * piece, piece), piece), :]
    for d in range(1, nt):
        summed = summed + rs_buf[lax.rem(tpos + d, nt)]
    logit = (
        jnp.sum(summed[:, :rank] * summed[:, rank : 2 * rank], axis=1, keepdims=True)
        + summed[:, 2 * rank :]
    )
    logits_ref[...] = logit
    error = sigmoid(logit) - label_ref[...]
    gath[me, tpos, :, :rank] = error * summed[:, :rank]
    gath[me, tpos, :, rank : 2 * rank] = error * summed[:, rank : 2 * rank]
    gath[me, tpos, :, 2 * rank :] = error

    def member_copy(d):
        return pltpu.make_async_remote_copy(
            src_ref=gath.at[me, tpos],
            dst_ref=gath.at[me, tpos],
            send_sem=gm_send.at[d],
            recv_sem=gm_recv.at[d],
            device_id={"member": lax.rem(me + d, n)},
            device_id_type=MESH,
        )

    for d in range(1, n):
        member_copy(d).start()
    for d in range(1, nt):
        tower_copy(d).wait_send()
    sent(me, True, True)
    for d in range(1, chips):

        @pl.when(chip >= d)
        def _():
            sent(me - 2 * d, True, False)

        @pl.when(chip + d < chips)
        def _():
            sent(me + 2 * d, False, True)

    for d in range(1, n):
        member_copy(d).wait_recv()

    def column_copy(d):
        return pltpu.make_async_remote_copy(
            src_ref=gath.at[:, tpos],
            dst_ref=gath.at[:, tpos],
            send_sem=gt_send.at[d],
            recv_sem=gt_recv.at[d],
            device_id={"tower": lax.rem(tpos + d, nt)},
            device_id_type=MESH,
        )

    for d in range(1, nt):
        column_copy(d).start()
    for d in range(1, nt):
        column_copy(d).wait_recv()
    store(gath, gath_out)
    for d in range(1, n):
        member_copy(d).wait_send()
    for d in range(1, nt):
        column_copy(d).wait_send()

    @pl.loop(0, total // chunk)
    def _(c):
        for t in range(towers):
            hidden_copy(t, c).wait()

    for copy in stores:
        copy.wait()


def update_kernel(
    dims,
    acc_ref,
    decayed_ref,
    first_ref,
    pooled_ref,
    gath_ref,
    w2h_ref,
    w2l_ref,
    lift_hbm,
    press_hbm,
    head_ref,
    hidden_hbm,
    counts_hbm,
    new_tables_ref,
    new_acc_ref,
    grad_first_ref,
    grad_second_ref,
    grad_lift_ref,
    grad_press_ref,
    lift,
    press,
    hidden,
    counts,
    act,
    gl,
    gp,
    gf,
    gsec,
    gt,
    load_sem,
    hidden_sem,
    counts_sem,
):
    n, nt = dims
    me = lax.axis_index("member")
    tpos = lax.axis_index("tower")
    towers, total, hid = hidden.shape
    width, rows = decayed_ref.shape[1:]
    outs = w2h_ref.shape[2]
    rank = lift.shape[1]
    flat = towers * outs
    own = total // n
    chunk = min(256, total)

    loads = []

    def load(source, target):
        loads.append(pltpu.make_async_copy(source, target, load_sem.at[len(loads)]))
        loads[-1].start()

    load(lift_hbm.at[pl.ds(tpos * flat, flat)], lift)
    load(press_hbm.at[pl.ds(tpos * flat, flat)], press)

    def hidden_copy(t, c):
        span = pl.ds(pl.multiple_of(c * chunk, chunk), chunk)
        return pltpu.make_async_copy(
            hidden_hbm.at[t, span], hidden.at[t, span], hidden_sem.at[t, c]
        )

    def counts_copy(t):
        return pltpu.make_async_copy(counts_hbm.at[t], counts.at[t], counts_sem.at[t])

    for t in range(towers):
        for c in range(total // chunk):
            hidden_copy(t, c).start()
        counts_copy(t).start()

    block_hid = hid // n
    window = max(block_hid, 128)
    start = pl.multiple_of((me * block_hid) // 128 * 128, 128)
    gf[...] = jnp.zeros_like(gf)
    gsec[...] = jnp.zeros_like(gsec)
    gl[...] = jnp.zeros_like(gl)
    gp[...] = jnp.zeros_like(gp)
    gt[...] = jnp.zeros_like(gt)
    members_here = chunk // own
    head = head_ref[:, pl.ds(pl.multiple_of(tpos * flat, flat), flat)]
    for copy in loads:
        copy.wait()
    lift_pair = split(lift[...])
    press_pair = split(press[...])

    for t in range(towers):
        counts_copy(t).wait()
        first = split(first_ref[:, t, :])

        @pl.loop(0, total // chunk)
        def _(c):
            hidden_copy(t, c).wait()
            span = pl.ds(pl.multiple_of(c * chunk, chunk), chunk)
            block = gath_ref[pl.ds(c * members_here, members_here)].reshape(chunk, 3 * rank)
            ep = split(block[:, :rank])
            eg = split(block[:, rank : 2 * rank])
            part = slice(t * outs, (t + 1) * outs)
            head_t = head[:, part]
            lift_t = tuple(x[part] for x in lift_pair)
            press_t = tuple(x[part] for x in press_pair)
            w2 = (w2h_ref[t], w2l_ref[t])
            error_all = block[:, 2 * rank : 2 * rank + 1]
            grad_out = head_t * (error_all + dot3(ep, lift_t, NT)) + dot3(eg, press_t, NT)
            h = hidden[t, span, :]
            sig = sigmoid(h)
            a = h * sig
            act[...] = a
            tower_out = dot3(split(a), w2)
            gl[part] += dot3(split((tower_out * head_t).T), ep)
            gp[part] += dot3(split(tower_out.T), eg)
            go = split(grad_out)
            gsec[t] += dot3(split(act[:, pl.ds(start, window)].T), go)
            grad_hidden = split(dot3(go, w2, NT) * (sig * (1.0 + h * (1.0 - sig))))
            pooled = pooled_ref[span, :].T[t * width : (t + 1) * width]
            gf[t] += dot3(split(pooled), grad_hidden)
            grad_pooled = dot3(first, grad_hidden, NT)
            both = dot1(jnp.concatenate(split(grad_pooled), axis=0), counts[t, span, :])
            gt[t] += both[:width] + both[width:]

        shift = pl.multiple_of(me * block_hid - start, min(block_hid, 128))
        grad_second_ref[:, t, :] = gsec[t, pl.ds(shift, block_hid), :]
        grad_first_ref[:, t, :] = gf[t]
        g = gt[t]
        value = acc_ref[t] + jnp.mean(g * g, axis=0, keepdims=True)
        new_acc_ref[t] = value
        new_tables_ref[t] = decayed_ref[t] - LEARN_RATE * g / (jnp.sqrt(value) + EPSILON)

    own_flat = pl.ds(pl.multiple_of(me * (flat // n), flat // n), flat // n)
    grad_lift_ref[...] = gl[own_flat]
    grad_press_ref[...] = gp[own_flat]


def per_device(n, nt, *args):
    bag_ids, touch_ids, elapsed, tables, accumulator, first, second, lift, press, head, labels = args
    towers, _, bags, total = bag_ids.shape
    rows, width = tables.shape[2:]
    fin, _, hid = first.shape
    outs = second.shape[2]
    rank = lift.shape[1]
    flat = towers * outs
    own = total // n
    piece = own // nt
    block_hid = hid // n
    window = max(block_hid, 128)
    me = lax.axis_index("member")
    tpos = lax.axis_index("tower")
    label = lax.dynamic_slice_in_dim(labels[0], tpos * piece, piece, 0).astype(F32)
    label = jnp.broadcast_to(label[:, None], (piece, rank))
    vmem = pl.BlockSpec(memory_space=pltpu.VMEM)
    anys = pl.BlockSpec(memory_space=pl.ANY)
    chunk = min(256, total)
    sem = pltpu.SemaphoreType.DMA
    lanes = towers * width
    shape = jax.ShapeDtypeStruct
    logits, decayed, pooled, hidden, gath, counts, w2h, w2l = pl.pallas_call(
        functools.partial(gather_kernel, (n, nt)),
        out_shape=(
            shape((piece, rank), F32),
            shape((towers, width, rows), F32),
            shape((total, lanes), F32),
            shape((towers, total, hid), F32),
            shape((n, nt, piece, 3 * rank), F32),
            shape((towers, total, rows), BF16),
            shape((towers, hid, outs), BF16),
            shape((towers, hid, outs), BF16),
        ),
        in_specs=[vmem] * 4 + [anys] * 4 + [vmem] * 2,
        out_specs=[vmem] * 2 + [anys] * 6,
        scratch_shapes=[
            pltpu.VMEM((towers, fin, hid), BF16),
            pltpu.VMEM((towers, fin, hid), BF16),
            pltpu.VMEM((towers, hid, outs), F32),
            pltpu.VMEM((towers, hid, outs), BF16),
            pltpu.VMEM((towers, hid, outs), BF16),
            pltpu.VMEM((flat, rank), F32),
            pltpu.VMEM((flat, rank), F32),
            pltpu.VMEM((total, 128), F32),
            pltpu.VMEM((towers, total, rows), BF16),
            pltpu.VMEM((n, total, lanes), F32),
            pltpu.VMEM((towers, max(total, fin), hid), F32),
            pltpu.VMEM((own, 3 * rank), F32),
            pltpu.VMEM((nt, piece, 3 * rank), F32),
            pltpu.VMEM((n, nt, piece, 3 * rank), F32),
            sem((2 * towers + 2,)),
            sem((5,)),
            sem((towers, total // chunk)),
            sem((3, n)),
            sem((n,)),
            sem((nt,)),
            sem((nt,)),
            sem((n,)),
            sem((n,)),
            sem((nt,)),
            sem((nt,)),
        ],
        compiler_params=pltpu.CompilerParams(
            collective_id=0, has_side_effects=True, vmem_limit_bytes=67043328
        ),
    )(
        bag_ids[:, 0],
        touch_ids,
        elapsed,
        jnp.transpose(tables[:, 0], (0, 2, 1)),
        first,
        second,
        lift,
        press,
        head[None, :],
        label,
    )
    out = pl.pallas_call(
        functools.partial(update_kernel, (n, nt)),
        out_shape=(
            shape((towers, width, rows), F32),
            shape((towers, 1, rows), F32),
            shape((width, towers, hid), F32),
            shape((block_hid, towers, outs), F32),
            shape((flat // n, rank), F32),
            shape((flat // n, rank), F32),
        ),
        grid=(1,),
        in_specs=[vmem] * 2
        + [pl.BlockSpec((width, towers, hid), lambda i: (lax.axis_index("member"), 0, 0))]
        + [vmem] * 4
        + [anys] * 2
        + [vmem]
        + [anys] * 2,
        out_specs=[vmem] * 6,
        scratch_shapes=[
            pltpu.VMEM((flat, rank), F32),
            pltpu.VMEM((flat, rank), F32),
            pltpu.VMEM((towers, total, hid), F32),
            pltpu.VMEM((towers, total, rows), BF16),
            pltpu.VMEM((chunk, hid), F32),
            pltpu.VMEM((flat, rank), F32),
            pltpu.VMEM((flat, rank), F32),
            pltpu.VMEM((towers, width, hid), F32),
            pltpu.VMEM((towers, window, outs), F32),
            pltpu.VMEM((towers, width, rows), F32),
            sem((2,)),
            sem((towers, total // chunk)),
            sem((towers,)),
        ],
        compiler_params=pltpu.CompilerParams(vmem_limit_bytes=67043328),
    )(
        accumulator,
        decayed,
        first,
        pooled,
        gath,
        w2h,
        w2l,
        lift,
        press,
        head[None, :],
        hidden,
        counts,
    )
    new_tables, new_acc, grad_first, grad_second, grad_lift, grad_press = out
    return (
        jnp.transpose(new_tables, (0, 2, 1))[:, None],
        new_acc,
        grad_first,
        grad_second,
        grad_lift,
        grad_press,
        logits[:, 0][None, :],
    )


def solution(mesh):
    placed = (
        P("tower", "member", None, None),
        P("tower", "member", None),
        P("tower", "member", None),
        P("tower", "member", None, None),
        P("tower", "member", None),
        P(None, "tower", None),
        P(None, "tower", None),
        P(),
        P(),
        P(),
        P("member", None),
    )
    return jax.shard_map(
        functools.partial(per_device, mesh.shape["member"], mesh.shape["tower"]),
        mesh=mesh,
        in_specs=placed,
        out_specs=(
            P("tower", "member", None, None),
            P("tower", "member", None),
            P("member", "tower", None),
            P("member", "tower", None),
            P(("tower", "member"), None),
            P(("tower", "member"), None),
            P("member", "tower"),
        ),
        check_vma=False,
    )
```

```python
import functools
import math

import jax
import jax.numpy as jnp
from jax import lax
from jax.experimental import pallas as pl
from jax.experimental.pallas import tpu as pltpu
from jax.sharding import PartitionSpec as P

MESH = pl.DeviceIdType.MESH
DECAY_RATE = 0.98
LEARN_RATE = 1.0
EPSILON = 1e-08
F32 = jnp.float32
BF16 = jnp.bfloat16
NN = (((1,), (0,)), ((), ()))
NT = (((1,), (1,)), ((), ()))


def split(x):
    hi = x.astype(BF16)
    return hi, (x - hi.astype(F32)).astype(BF16)


def dot1(a, b, dims=NN):
    return lax.dot_general(a, b, dims, preferred_element_type=F32)


def dot3(a, b, dims=NN):
    (ah, al), (bh, bl) = a, b
    return dot1(ah, bh, dims) + (dot1(ah, bl, dims) + dot1(al, bh, dims))


def sigmoid(x):
    return 1.0 / (1.0 + jnp.exp(-x))


def gather_kernel(
    dims,
    bag_ref,
    touch_ref,
    elapsed_ref,
    tables_ref,
    first_hbm,
    second_hbm,
    lift_hbm,
    press_hbm,
    head_ref,
    label_ref,
    logits_ref,
    decayed_ref,
    pooled_out,
    hidden_out,
    gath_out,
    counts_out,
    w2h_out,
    w2l_out,
    tower_out_hbm,
    w1h,
    w1l,
    w2f,
    w2h,
    w2l,
    lift,
    press,
    cols,
    counts_ref,
    feats,
    hidden,
    tower_out,
    stats,
    rs_buf,
    gath,
    load_sem,
    store_sem,
    hidden_sem,
    ag_send,
    ag_recv,
    rs_send,
    rs_recv,
    gm_send,
    gm_recv,
    gt_send,
    gt_recv,
):
    n, nt = dims
    me = lax.axis_index("member")
    tpos = lax.axis_index("tower")
    towers, bags, total = bag_ref.shape
    width, rows = tables_ref.shape[1:]
    touches = touch_ref.shape[2]
    hid, outs = w2h.shape[1:]
    fin = w1h.shape[1]
    rank = lift.shape[1]
    flat = towers * outs
    own = total // n
    piece = own // nt
    chunk = min(256, total)
    chips = n // 2
    chip, core = me // 2, lax.rem(me, 2)

    loads = []

    def load(source, target):
        loads.append(pltpu.make_async_copy(source, target, load_sem.at[len(loads)]))
        loads[-1].start()

    for t in range(towers):
        load(first_hbm.at[:, t, :], hidden.at[t, :fin])
        load(second_hbm.at[:, t, :], w2f.at[t])
    load(lift_hbm.at[pl.ds(tpos * flat, flat)], lift)
    load(press_hbm.at[pl.ds(tpos * flat, flat)], press)

    barrier = pltpu.get_barrier_semaphore()
    for d in range(1, n):
        pl.semaphore_signal(
            barrier, inc=1, device_id={"member": lax.rem(me + d, n)}, device_id_type=MESH
        )
    for d in range(1, nt):
        pl.semaphore_signal(
            barrier, inc=1, device_id={"tower": lax.rem(tpos + d, nt)}, device_id_type=MESH
        )

    stack = [bag_ref[t].astype(F32) for t in range(towers)]
    stack.append(jnp.zeros((128 - towers * bags, total), F32))
    cols[...] = jnp.concatenate(stack, axis=0).T
    stack = []
    for t in range(towers):
        stack.append(touch_ref[t].astype(F32))
        stack.append(jnp.exp(elapsed_ref[t].astype(F32) * math.log(DECAY_RATE)))
    stack.append(jnp.zeros((128 - 2 * towers, touches), F32))
    owed = jnp.concatenate(stack, axis=0).T
    pairs = []
    place = lax.broadcasted_iota(jnp.int32, (touches, rows), 1).astype(F32)
    for t in range(towers):
        ids, rates = owed[:, 2 * t : 2 * t + 1], owed[:, 2 * t + 1 : 2 * t + 2]
        chosen = jnp.sum(jnp.where(place == ids, rates, 0.0), axis=0, keepdims=True)
        decayed = tables_ref[t] * jnp.where(chosen > 0.0, chosen, 1.0)
        decayed_ref[t] = decayed
        pairs.append(jnp.concatenate(split(decayed), axis=0))
    for c in range(total // chunk):
        span = pl.ds(c * chunk, chunk)
        place = lax.broadcasted_iota(jnp.int32, (chunk, rows), 1).astype(F32)
        pooled = []
        for t in range(towers):
            counts = jnp.zeros((chunk, rows), F32)
            for b in range(bags):
                k = t * bags + b
                counts = counts + jnp.where(place == cols[span, k : k + 1], 1.0, 0.0)
            counts = counts.astype(BF16)
            counts_ref[t, span, :] = counts
            both = dot1(counts, pairs[t], NT)
            pooled.append(both[:, :width] + both[:, width:])
        feats[me, span, :] = jnp.concatenate(pooled, axis=1)

    pl.semaphore_wait(barrier, n - 1 + nt - 1)

    def block_copy(block, lane, target):
        return pltpu.make_async_remote_copy(
            src_ref=feats.at[block],
            dst_ref=feats.at[block],
            send_sem=ag_send.at[lane, block],
            recv_sem=ag_recv.at[block],
            device_id={"member": target},
            device_id_type=MESH,
        )

    def pass_on(block, right, left):
        if right:

            @pl.when(chip + 1 < chips)
            def _():
                block_copy(block, 0, me + 2).start()

        if left:

            @pl.when(chip > 0)
            def _():
                block_copy(block, 1, me - 2).start()

        block_copy(block, 2, me + 1 - 2 * core).start()

    def sent(block, right, left):
        if right:

            @pl.when(chip + 1 < chips)
            def _():
                block_copy(block, 0, me + 2).wait_send()

        if left:

            @pl.when(chip > 0)
            def _():
                block_copy(block, 1, me - 2).wait_send()

        block_copy(block, 2, me + 1 - 2 * core).wait_send()

    pass_on(me, True, True)

    stores = []

    def store(source, target):
        stores.append(pltpu.make_async_copy(source, target, store_sem.at[len(stores)]))
        stores[-1].start()

    store(counts_ref, counts_out)

    for copy in loads:
        copy.wait()
    for t in range(towers):

        @pl.loop(0, fin // 64)
        def _(i):
            span = pl.ds(pl.multiple_of(i * 64, 64), 64)
            w1h[t, span, :], w1l[t, span, :] = split(hidden[t, span, :])

        @pl.loop(0, hid // 128)
        def _(i):
            span = pl.ds(pl.multiple_of(i * 128, 128), 128)
            w2h[t, span, :], w2l[t, span, :] = split(w2f[t, span, :])

    store(w2h, w2h_out)
    store(w2l, w2l_out)
    store(feats.at[me], pooled_out)

    def accumulate(source, fresh):
        block_copy(2 * source + 1 - core, 0, me).wait_recv()
        ins = pl.ds(pl.multiple_of(source * 2 * width, 2 * width), 2 * width)

        @pl.loop(0, total // chunk)
        def _(c):
            span = pl.ds(pl.multiple_of(c * chunk, chunk), chunk)
            even, odd = feats[2 * source, span, :], feats[2 * source + 1, span, :]
            for t in range(towers):
                part = slice(t * width, (t + 1) * width)
                x = jnp.concatenate([even[:, part], odd[:, part]], axis=1)
                h = dot3(split(x), (w1h[t, ins, :], w1l[t, ins, :]))
                if fresh:
                    hidden[t, span, :] = h
                else:
                    hidden[t, span, :] += h

    accumulate(chip, True)
    for d in range(1, chips):

        @pl.when(chip >= d)
        def _():
            block = me - 2 * d
            block_copy(block, 0, me).wait_recv()
            pass_on(block, True, False)

        @pl.when(chip + d < chips)
        def _():
            block = me + 2 * d
            block_copy(block, 0, me).wait_recv()
            pass_on(block, False, True)

        @pl.when(chip >= d)
        def _():
            accumulate(chip - d, False)

        @pl.when(chip + d < chips)
        def _():
            accumulate(chip + d, False)

    def hidden_copy(t):
        return pltpu.make_async_copy(hidden.at[t, :total], hidden_out.at[t], hidden_sem.at[t])

    for t in range(towers):
        hidden_copy(t).start()

    head = head_ref[:, pl.ds(pl.multiple_of(tpos * flat, flat), flat)]

    mine = pl.ds(pl.multiple_of(me * own, own), own)
    flat_out = []
    for t in range(towers):
        h = hidden[t, mine, :]
        flat_out.append(dot3(split(h * sigmoid(h)), (w2h[t], w2l[t])))
    flat_out = jnp.concatenate(flat_out, axis=1)
    weighted = flat_out * head
    stats[:, :rank] = dot3(split(flat_out), split(press[...]))
    stats[:, rank : 2 * rank] = dot3(split(weighted), split(lift[...]))
    stats[:, 2 * rank :] = jnp.broadcast_to(
        jnp.sum(weighted, axis=1, keepdims=True), (own, rank)
    )

    def tower_copy(d):
        other = lax.rem(tpos + d, nt)
        return pltpu.make_async_remote_copy(
            src_ref=stats.at[pl.ds(pl.multiple_of(other * piece, piece), piece)],
            dst_ref=rs_buf.at[tpos],
            send_sem=rs_send.at[d],
            recv_sem=rs_recv.at[d],
            device_id={"tower": other},
            device_id_type=MESH,
        )

    for d in range(1, nt):
        tower_copy(d).start()

    def tower_chunks(t):
        @pl.loop(0, total // chunk)
        def _(c):
            span = pl.ds(pl.multiple_of(c * chunk, chunk), chunk)
            h = hidden[t, span, :]
            tower_out[t, span, :] = dot3(split(h * sigmoid(h)), (w2h[t], w2l[t]))

        store(tower_out.at[t], tower_out_hbm.at[t])

    tower_chunks(0)

    for d in range(1, nt):
        tower_copy(d).wait_recv()
    summed = stats[pl.ds(pl.multiple_of(tpos * piece, piece), piece), :]
    for d in range(1, nt):
        summed = summed + rs_buf[lax.rem(tpos + d, nt)]
    logit = (
        jnp.sum(summed[:, :rank] * summed[:, rank : 2 * rank], axis=1, keepdims=True)
        + summed[:, 2 * rank :]
    )
    logits_ref[...] = logit
    place = lax.broadcasted_iota(jnp.int32, (piece, own), 1)
    wanted = lax.broadcasted_iota(jnp.int32, (piece, own), 0) + tpos * piece
    clicks = jnp.where(place == wanted, label_ref[...].astype(F32), 0.0)
    error = sigmoid(logit) - jnp.sum(clicks, axis=1, keepdims=True)
    gath[me, tpos, :, :rank] = error * summed[:, :rank]
    gath[me, tpos, :, rank : 2 * rank] = error * summed[:, rank : 2 * rank]
    gath[me, tpos, :, 2 * rank :] = error

    def member_copy(d):
        return pltpu.make_async_remote_copy(
            src_ref=gath.at[me, tpos],
            dst_ref=gath.at[me, tpos],
            send_sem=gm_send.at[d],
            recv_sem=gm_recv.at[d],
            device_id={"member": lax.rem(me + d, n)},
            device_id_type=MESH,
        )

    for d in range(1, n):
        member_copy(d).start()
    for t in range(1, towers):
        tower_chunks(t)
    for d in range(1, nt):
        tower_copy(d).wait_send()
    sent(me, True, True)
    for d in range(1, chips):

        @pl.when(chip >= d)
        def _():
            sent(me - 2 * d, True, False)

        @pl.when(chip + d < chips)
        def _():
            sent(me + 2 * d, False, True)

    for d in range(1, n):
        member_copy(d).wait_recv()

    def column_copy(d):
        return pltpu.make_async_remote_copy(
            src_ref=gath.at[:, tpos],
            dst_ref=gath.at[:, tpos],
            send_sem=gt_send.at[d],
            recv_sem=gt_recv.at[d],
            device_id={"tower": lax.rem(tpos + d, nt)},
            device_id_type=MESH,
        )

    for d in range(1, nt):
        column_copy(d).start()
    for d in range(1, nt):
        column_copy(d).wait_recv()
    store(gath, gath_out)
    for d in range(1, n):
        member_copy(d).wait_send()
    for d in range(1, nt):
        column_copy(d).wait_send()

    for t in range(towers):
        hidden_copy(t).wait()
    for copy in stores:
        copy.wait()


def update_kernel(
    dims,
    logits_ref,
    tower_out_ref,
    acc_ref,
    decayed_ref,
    first_ref,
    pooled_ref,
    gath_ref,
    w2h_ref,
    w2l_ref,
    lift_hbm,
    press_hbm,
    head_ref,
    hidden_hbm,
    counts_hbm,
    new_tables_ref,
    new_acc_ref,
    grad_first_ref,
    grad_second_ref,
    grad_lift_ref,
    grad_press_ref,
    logits_out_ref,
    lift,
    press,
    hidden,
    counts,
    act,
    gl,
    gp,
    gf,
    gsec,
    gt,
    load_sem,
    hidden_sem,
    counts_sem,
):
    n, nt = dims
    me = lax.axis_index("member")
    tpos = lax.axis_index("tower")
    towers, total, hid = hidden.shape
    width, rows = decayed_ref.shape[1:]
    outs = w2h_ref.shape[2]
    rank = lift.shape[1]
    flat = towers * outs
    own = total // n
    chunk = min(256, total)

    loads = []

    def load(source, target):
        loads.append(pltpu.make_async_copy(source, target, load_sem.at[len(loads)]))
        loads[-1].start()

    load(lift_hbm.at[pl.ds(tpos * flat, flat)], lift)
    load(press_hbm.at[pl.ds(tpos * flat, flat)], press)

    def hidden_copy(t, c):
        span = pl.ds(pl.multiple_of(c * chunk, chunk), chunk)
        return pltpu.make_async_copy(
            hidden_hbm.at[t, span], hidden.at[t, span], hidden_sem.at[t, c]
        )

    def counts_copy(t):
        return pltpu.make_async_copy(counts_hbm.at[t], counts.at[t], counts_sem.at[t])

    for t in range(towers):
        for c in range(total // chunk):
            hidden_copy(t, c).start()
        counts_copy(t).start()

    block_hid = hid // n
    window = max(block_hid, 128)
    start = pl.multiple_of((me * block_hid) // 128 * 128, 128)
    gf[...] = jnp.zeros_like(gf)
    gsec[...] = jnp.zeros_like(gsec)
    gl[...] = jnp.zeros_like(gl)
    gp[...] = jnp.zeros_like(gp)
    gt[...] = jnp.zeros_like(gt)
    members_here = chunk // own
    head = head_ref[:, pl.ds(pl.multiple_of(tpos * flat, flat), flat)]
    for copy in loads:
        copy.wait()
    lift_pair = split(lift[...])
    press_pair = split(press[...])

    for t in range(towers):
        counts_copy(t).wait()
        first = split(first_ref[:, t, :])

        @pl.loop(0, total // chunk)
        def _(c):
            hidden_copy(t, c).wait()
            span = pl.ds(pl.multiple_of(c * chunk, chunk), chunk)
            block = gath_ref[pl.ds(c * members_here, members_here)].reshape(chunk, 3 * rank)
            ep = split(block[:, :rank])
            eg = split(block[:, rank : 2 * rank])
            part = slice(t * outs, (t + 1) * outs)
            head_t = head[:, part]
            lift_t = tuple(x[part] for x in lift_pair)
            press_t = tuple(x[part] for x in press_pair)
            w2 = (w2h_ref[t], w2l_ref[t])
            error_all = block[:, 2 * rank : 2 * rank + 1]
            grad_out = head_t * (error_all + dot3(ep, lift_t, NT)) + dot3(eg, press_t, NT)
            h = hidden[t, span, :]
            sig = sigmoid(h)
            a = h * sig
            act[...] = a
            tower_out = tower_out_ref[t, span, :]
            gl[part] += dot3(split((tower_out * head_t).T), ep)
            gp[part] += dot3(split(tower_out.T), eg)
            go = split(grad_out)
            gsec[t] += dot3(split(act[:, pl.ds(start, window)].T), go)
            grad_hidden = split(dot3(go, w2, NT) * (sig * (1.0 + h * (1.0 - sig))))
            pooled = pooled_ref[span, :].T[t * width : (t + 1) * width]
            gf[t] += dot3(split(pooled), grad_hidden)
            grad_pooled = dot3(first, grad_hidden, NT)
            both = dot1(jnp.concatenate(split(grad_pooled), axis=0), counts[t, span, :])
            gt[t] += both[:width] + both[width:]

        shift = pl.multiple_of(me * block_hid - start, min(block_hid, 128))
        grad_second_ref[:, t, :] = gsec[t, pl.ds(shift, block_hid), :]
        grad_first_ref[:, t, :] = gf[t]
        g = gt[t]
        value = acc_ref[t] + jnp.mean(g * g, axis=0, keepdims=True)
        new_acc_ref[t] = value
        new_tables_ref[t] = decayed_ref[t] - LEARN_RATE * g / (jnp.sqrt(value) + EPSILON)

    own_flat = pl.ds(pl.multiple_of(me * (flat // n), flat // n), flat // n)
    grad_lift_ref[...] = gl[own_flat]
    grad_press_ref[...] = gp[own_flat]
    piece = logits_ref.shape[0]
    place = lax.broadcasted_iota(jnp.int32, (piece, piece), 1)
    wanted = lax.broadcasted_iota(jnp.int32, (piece, piece), 0)
    values = jnp.where(place == wanted, logits_ref[:, :1], 0.0)
    logits_out_ref[...] = jnp.sum(values, axis=0, keepdims=True)


def per_device(n, nt, *args):
    bag_ids, touch_ids, elapsed, tables, accumulator, first, second, lift, press, head, labels = args
    towers, _, bags, total = bag_ids.shape
    rows, width = tables.shape[2:]
    fin, _, hid = first.shape
    outs = second.shape[2]
    rank = lift.shape[1]
    flat = towers * outs
    own = total // n
    piece = own // nt
    block_hid = hid // n
    window = max(block_hid, 128)
    vmem = pl.BlockSpec(memory_space=pltpu.VMEM)
    anys = pl.BlockSpec(memory_space=pl.ANY)
    chunk = min(256, total)
    sem = pltpu.SemaphoreType.DMA
    lanes = towers * width
    shape = jax.ShapeDtypeStruct
    logits, decayed, pooled, hidden, gath, counts, w2h, w2l, tower_out = pl.pallas_call(
        functools.partial(gather_kernel, (n, nt)),
        out_shape=(
            shape((piece, rank), F32),
            shape((towers, width, rows), F32),
            shape((total, lanes), F32),
            shape((towers, total, hid), F32),
            shape((n, nt, piece, 3 * rank), F32),
            shape((towers, total, rows), BF16),
            shape((towers, hid, outs), BF16),
            shape((towers, hid, outs), BF16),
            shape((towers, total, outs), F32),
        ),
        in_specs=[vmem] * 4 + [anys] * 4 + [vmem] * 2,
        out_specs=[vmem] * 2 + [anys] * 7,
        scratch_shapes=[
            pltpu.VMEM((towers, fin, hid), BF16),
            pltpu.VMEM((towers, fin, hid), BF16),
            pltpu.VMEM((towers, hid, outs), F32),
            pltpu.VMEM((towers, hid, outs), BF16),
            pltpu.VMEM((towers, hid, outs), BF16),
            pltpu.VMEM((flat, rank), F32),
            pltpu.VMEM((flat, rank), F32),
            pltpu.VMEM((total, 128), F32),
            pltpu.VMEM((towers, total, rows), BF16),
            pltpu.VMEM((n, total, lanes), F32),
            pltpu.VMEM((towers, max(total, fin), hid), F32),
            pltpu.VMEM((towers, total, outs), F32),
            pltpu.VMEM((own, 3 * rank), F32),
            pltpu.VMEM((nt, piece, 3 * rank), F32),
            pltpu.VMEM((n, nt, piece, 3 * rank), F32),
            sem((2 * towers + 2,)),
            sem((4 + towers + 1,)),
            sem((towers,)),
            sem((3, n)),
            sem((n,)),
            sem((nt,)),
            sem((nt,)),
            sem((n,)),
            sem((n,)),
            sem((nt,)),
            sem((nt,)),
        ],
        compiler_params=pltpu.CompilerParams(
            collective_id=0, has_side_effects=True, vmem_limit_bytes=67043328
        ),
    )(
        bag_ids[:, 0],
        touch_ids,
        elapsed,
        jnp.transpose(tables[:, 0], (0, 2, 1)),
        first,
        second,
        lift,
        press,
        head[None, :],
        labels,
    )
    out = pl.pallas_call(
        functools.partial(update_kernel, (n, nt)),
        out_shape=(
            shape((towers, width, rows), F32),
            shape((towers, 1, rows), F32),
            shape((width, towers, hid), F32),
            shape((block_hid, towers, outs), F32),
            shape((flat // n, rank), F32),
            shape((flat // n, rank), F32),
            shape((1, piece), F32),
        ),
        grid=(1,),
        in_specs=[vmem] * 4
        + [pl.BlockSpec((width, towers, hid), lambda i: (lax.axis_index("member"), 0, 0))]
        + [vmem] * 4
        + [anys] * 2
        + [vmem]
        + [anys] * 2,
        out_specs=[vmem] * 7,
        scratch_shapes=[
            pltpu.VMEM((flat, rank), F32),
            pltpu.VMEM((flat, rank), F32),
            pltpu.VMEM((towers, total, hid), F32),
            pltpu.VMEM((towers, total, rows), BF16),
            pltpu.VMEM((chunk, hid), F32),
            pltpu.VMEM((flat, rank), F32),
            pltpu.VMEM((flat, rank), F32),
            pltpu.VMEM((towers, width, hid), F32),
            pltpu.VMEM((towers, window, outs), F32),
            pltpu.VMEM((towers, width, rows), F32),
            sem((2,)),
            sem((towers, total // chunk)),
            sem((towers,)),
        ],
        compiler_params=pltpu.CompilerParams(vmem_limit_bytes=67043328),
    )(
        logits,
        tower_out,
        accumulator,
        decayed,
        first,
        pooled,
        gath,
        w2h,
        w2l,
        lift,
        press,
        head[None, :],
        hidden,
        counts,
    )
    new_tables, new_acc, grad_first, grad_second, grad_lift, grad_press, logits = out
    return (
        jnp.transpose(new_tables, (0, 2, 1))[:, None],
        new_acc,
        grad_first,
        grad_second,
        grad_lift,
        grad_press,
        logits,
    )


def solution(mesh):
    placed = (
        P("tower", "member", None, None),
        P("tower", "member", None),
        P("tower", "member", None),
        P("tower", "member", None, None),
        P("tower", "member", None),
        P(None, "tower", None),
        P(None, "tower", None),
        P(),
        P(),
        P(),
        P("member", None),
    )
    return jax.shard_map(
        functools.partial(per_device, mesh.shape["member"], mesh.shape["tower"]),
        mesh=mesh,
        in_specs=placed,
        out_specs=(
            P("tower", "member", None, None),
            P("tower", "member", None),
            P("member", "tower", None),
            P("member", "tower", None),
            P(("tower", "member"), None),
            P(("tower", "member"), None),
            P("member", "tower"),
        ),
        check_vma=False,
    )
```

```python
import functools
import math

import jax
import jax.numpy as jnp
from jax import lax
from jax.experimental import pallas as pl
from jax.experimental.pallas import tpu as pltpu
from jax.sharding import PartitionSpec as P

MESH = pl.DeviceIdType.MESH
DECAY_RATE = 0.98
LEARN_RATE = 1.0
EPSILON = 1e-08
F32 = jnp.float32
BF16 = jnp.bfloat16
NN = (((1,), (0,)), ((), ()))
NT = (((1,), (1,)), ((), ()))


def split(x):
    hi = x.astype(BF16)
    return hi, (x - hi.astype(F32)).astype(BF16)


def dot1(a, b, dims=NN):
    return lax.dot_general(a, b, dims, preferred_element_type=F32)


def dot3(a, b, dims=NN):
    (ah, al), (bh, bl) = a, b
    return dot1(ah, bh, dims) + (dot1(ah, bl, dims) + dot1(al, bh, dims))


def sigmoid(x):
    return 1.0 / (1.0 + jnp.exp(-x))


def gather_kernel(
    dims,
    bag_ref,
    touch_ref,
    elapsed_ref,
    tables_ref,
    first_hbm,
    second_hbm,
    lift_hbm,
    press_hbm,
    head_ref,
    label_ref,
    logits_ref,
    decayed_ref,
    pooled_out,
    hidden_out,
    gath_out,
    counts_out,
    w2h_out,
    w2l_out,
    tower_out_hbm,
    w1h,
    w1l,
    w2f,
    w2h,
    w2l,
    lift,
    press,
    cols,
    counts_ref,
    feats,
    hidden,
    tower_out,
    own_feats,
    oa_send,
    oa_recv,
    stats,
    rs_buf,
    gath,
    load_sem,
    store_sem,
    hidden_sem,
    ag_send,
    ag_recv,
    rs_send,
    rs_recv,
    gm_send,
    gm_recv,
    gt_send,
    gt_recv,
):
    n, nt = dims
    me = lax.axis_index("member")
    tpos = lax.axis_index("tower")
    towers, bags, total = bag_ref.shape
    width, rows = tables_ref.shape[1:]
    touches = touch_ref.shape[2]
    hid, outs = w2h.shape[1:]
    fin = w1h.shape[1]
    rank = lift.shape[1]
    flat = towers * outs
    own = total // n
    piece = own // nt
    chunk = min(256, total)
    chips = n // 2
    chip, core = me // 2, lax.rem(me, 2)

    loads = []

    def load(source, target):
        loads.append(pltpu.make_async_copy(source, target, load_sem.at[len(loads)]))
        loads[-1].start()

    for t in range(towers):
        load(first_hbm.at[:, t, :], hidden.at[t, :fin])
        load(second_hbm.at[:, t, :], w2f.at[t])
    load(lift_hbm.at[pl.ds(tpos * flat, flat)], lift)
    load(press_hbm.at[pl.ds(tpos * flat, flat)], press)

    barrier = pltpu.get_barrier_semaphore()
    for d in range(1, n):
        pl.semaphore_signal(
            barrier, inc=1, device_id={"member": lax.rem(me + d, n)}, device_id_type=MESH
        )
    for d in range(1, nt):
        pl.semaphore_signal(
            barrier, inc=1, device_id={"tower": lax.rem(tpos + d, nt)}, device_id_type=MESH
        )

    stack = [bag_ref[t].astype(F32) for t in range(towers)]
    stack.append(jnp.zeros((128 - towers * bags, total), F32))
    cols[...] = jnp.concatenate(stack, axis=0).T
    stack = []
    for t in range(towers):
        stack.append(touch_ref[t].astype(F32))
        stack.append(jnp.exp(elapsed_ref[t].astype(F32) * math.log(DECAY_RATE)))
    stack.append(jnp.zeros((128 - 2 * towers, touches), F32))
    owed = jnp.concatenate(stack, axis=0).T
    pairs = []
    place = lax.broadcasted_iota(jnp.int32, (touches, rows), 1).astype(F32)
    for t in range(towers):
        ids, rates = owed[:, 2 * t : 2 * t + 1], owed[:, 2 * t + 1 : 2 * t + 2]
        chosen = jnp.sum(jnp.where(place == ids, rates, 0.0), axis=0, keepdims=True)
        decayed = tables_ref[t] * jnp.where(chosen > 0.0, chosen, 1.0)
        decayed_ref[t] = decayed
        pairs.append(jnp.concatenate(split(decayed), axis=0))
    for c in range(total // chunk):
        span = pl.ds(c * chunk, chunk)
        place = lax.broadcasted_iota(jnp.int32, (chunk, rows), 1).astype(F32)
        pooled = []
        for t in range(towers):
            counts = jnp.zeros((chunk, rows), F32)
            for b in range(bags):
                k = t * bags + b
                counts = counts + jnp.where(place == cols[span, k : k + 1], 1.0, 0.0)
            counts = counts.astype(BF16)
            counts_ref[t, span, :] = counts
            both = dot1(counts, pairs[t], NT)
            pooled.append(both[:, :width] + both[:, width:])
        feats[me, span, :] = jnp.concatenate(pooled, axis=1)

    pl.semaphore_wait(barrier, n - 1 + nt - 1)

    def block_copy(block, lane, target):
        return pltpu.make_async_remote_copy(
            src_ref=feats.at[block],
            dst_ref=feats.at[block],
            send_sem=ag_send.at[lane, block],
            recv_sem=ag_recv.at[block],
            device_id={"member": target},
            device_id_type=MESH,
        )

    def pass_on(block, right, left):
        if right:

            @pl.when(chip + 1 < chips)
            def _():
                block_copy(block, 0, me + 2).start()

        if left:

            @pl.when(chip > 0)
            def _():
                block_copy(block, 1, me - 2).start()

        block_copy(block, 2, me + 1 - 2 * core).start()

    def sent(block, right, left):
        if right:

            @pl.when(chip + 1 < chips)
            def _():
                block_copy(block, 0, me + 2).wait_send()

        if left:

            @pl.when(chip > 0)
            def _():
                block_copy(block, 1, me - 2).wait_send()

        block_copy(block, 2, me + 1 - 2 * core).wait_send()

    def own_copy(d):
        other = lax.rem(me + d, n)
        return pltpu.make_async_remote_copy(
            src_ref=feats.at[me, pl.ds(pl.multiple_of(other * own, own), own)],
            dst_ref=own_feats.at[me],
            send_sem=oa_send.at[d],
            recv_sem=oa_recv.at[d],
            device_id={"member": other},
            device_id_type=MESH,
        )

    for d in range(1, n):
        own_copy(d).start()
    own_feats[me] = feats[me, pl.ds(pl.multiple_of(me * own, own), own), :]
    pass_on(me, True, True)

    stores = []

    def store(source, target):
        stores.append(pltpu.make_async_copy(source, target, store_sem.at[len(stores)]))
        stores[-1].start()

    store(counts_ref, counts_out)

    for copy in loads:
        copy.wait()
    for t in range(towers):

        @pl.loop(0, fin // 64)
        def _(i):
            span = pl.ds(pl.multiple_of(i * 64, 64), 64)
            w1h[t, span, :], w1l[t, span, :] = split(hidden[t, span, :])

        @pl.loop(0, hid // 128)
        def _(i):
            span = pl.ds(pl.multiple_of(i * 128, 128), 128)
            w2h[t, span, :], w2l[t, span, :] = split(w2f[t, span, :])

    store(w2h, w2h_out)
    store(w2l, w2l_out)
    store(feats.at[me], pooled_out)

    head = head_ref[:, pl.ds(pl.multiple_of(tpos * flat, flat), flat)]

    for d in range(1, n):
        own_copy(d).wait_recv()
    flat_out = []
    for t in range(towers):
        part = slice(t * width, (t + 1) * width)
        x = jnp.concatenate([own_feats[j, :, part] for j in range(n)], axis=1)
        h = dot3(split(x), (w1h[t], w1l[t]))
        flat_out.append(dot3(split(h * sigmoid(h)), (w2h[t], w2l[t])))
    flat_out = jnp.concatenate(flat_out, axis=1)
    weighted = flat_out * head
    stats[:, :rank] = dot3(split(flat_out), split(press[...]))
    stats[:, rank : 2 * rank] = dot3(split(weighted), split(lift[...]))
    stats[:, 2 * rank :] = jnp.broadcast_to(
        jnp.sum(weighted, axis=1, keepdims=True), (own, rank)
    )

    def tower_copy(d):
        other = lax.rem(tpos + d, nt)
        return pltpu.make_async_remote_copy(
            src_ref=stats.at[pl.ds(pl.multiple_of(other * piece, piece), piece)],
            dst_ref=rs_buf.at[tpos],
            send_sem=rs_send.at[d],
            recv_sem=rs_recv.at[d],
            device_id={"tower": other},
            device_id_type=MESH,
        )

    for d in range(1, nt):
        tower_copy(d).start()

    def member_copy(d):
        return pltpu.make_async_remote_copy(
            src_ref=gath.at[me, tpos],
            dst_ref=gath.at[me, tpos],
            send_sem=gm_send.at[d],
            recv_sem=gm_recv.at[d],
            device_id={"member": lax.rem(me + d, n)},
            device_id_type=MESH,
        )

    def settle():
        for d in range(1, nt):
            tower_copy(d).wait_recv()
        summed = stats[pl.ds(pl.multiple_of(tpos * piece, piece), piece), :]
        for d in range(1, nt):
            summed = summed + rs_buf[lax.rem(tpos + d, nt)]
        logit = (
            jnp.sum(summed[:, :rank] * summed[:, rank : 2 * rank], axis=1, keepdims=True)
            + summed[:, 2 * rank :]
        )
        logits_ref[...] = logit
        place = lax.broadcasted_iota(jnp.int32, (piece, own), 1)
        wanted = lax.broadcasted_iota(jnp.int32, (piece, own), 0) + tpos * piece
        clicks = jnp.where(place == wanted, label_ref[...].astype(F32), 0.0)
        error = sigmoid(logit) - jnp.sum(clicks, axis=1, keepdims=True)
        gath[me, tpos, :, :rank] = error * summed[:, :rank]
        gath[me, tpos, :, rank : 2 * rank] = error * summed[:, rank : 2 * rank]
        gath[me, tpos, :, 2 * rank :] = error

        for d in range(1, n):
            member_copy(d).start()

    def accumulate(source, fresh):
        block_copy(2 * source + 1 - core, 0, me).wait_recv()
        ins = pl.ds(pl.multiple_of(source * 2 * width, 2 * width), 2 * width)

        @pl.loop(0, total // chunk)
        def _(c):
            span = pl.ds(pl.multiple_of(c * chunk, chunk), chunk)
            even, odd = feats[2 * source, span, :], feats[2 * source + 1, span, :]
            for t in range(towers):
                part = slice(t * width, (t + 1) * width)
                x = jnp.concatenate([even[:, part], odd[:, part]], axis=1)
                h = dot3(split(x), (w1h[t, ins, :], w1l[t, ins, :]))
                if fresh:
                    hidden[t, span, :] = h
                else:
                    hidden[t, span, :] += h

    accumulate(chip, True)
    for d in range(1, chips):

        @pl.when(chip >= d)
        def _():
            block = me - 2 * d
            block_copy(block, 0, me).wait_recv()
            pass_on(block, True, False)

        @pl.when(chip + d < chips)
        def _():
            block = me + 2 * d
            block_copy(block, 0, me).wait_recv()
            pass_on(block, False, True)

        @pl.when(chip >= d)
        def _():
            accumulate(chip - d, False)

        @pl.when(chip + d < chips)
        def _():
            accumulate(chip + d, False)

        if d == 1:
            settle()

    def hidden_copy(t):
        return pltpu.make_async_copy(hidden.at[t, :total], hidden_out.at[t], hidden_sem.at[t])

    for t in range(towers):
        hidden_copy(t).start()

    def tower_chunks(t):
        @pl.loop(0, total // chunk)
        def _(c):
            span = pl.ds(pl.multiple_of(c * chunk, chunk), chunk)
            h = hidden[t, span, :]
            tower_out[t, span, :] = dot3(split(h * sigmoid(h)), (w2h[t], w2l[t]))

        store(tower_out.at[t], tower_out_hbm.at[t])

    for d in range(1, n):
        member_copy(d).wait_recv()

    def column_copy(d):
        return pltpu.make_async_remote_copy(
            src_ref=gath.at[:, tpos],
            dst_ref=gath.at[:, tpos],
            send_sem=gt_send.at[d],
            recv_sem=gt_recv.at[d],
            device_id={"tower": lax.rem(tpos + d, nt)},
            device_id_type=MESH,
        )

    for d in range(1, nt):
        column_copy(d).start()
    for t in range(towers):
        tower_chunks(t)
    for d in range(1, nt):
        column_copy(d).wait_recv()
    store(gath, gath_out)
    for d in range(1, n):
        own_copy(d).wait_send()
    for d in range(1, nt):
        tower_copy(d).wait_send()
    sent(me, True, True)
    for d in range(1, chips):

        @pl.when(chip >= d)
        def _():
            sent(me - 2 * d, True, False)

        @pl.when(chip + d < chips)
        def _():
            sent(me + 2 * d, False, True)
    for d in range(1, n):
        member_copy(d).wait_send()
    for d in range(1, nt):
        column_copy(d).wait_send()

    for t in range(towers):
        hidden_copy(t).wait()
    for copy in stores:
        copy.wait()


def update_kernel(
    dims,
    logits_ref,
    tower_out_ref,
    acc_ref,
    decayed_ref,
    first_ref,
    pooled_ref,
    gath_ref,
    w2h_ref,
    w2l_ref,
    lift_hbm,
    press_hbm,
    head_ref,
    hidden_hbm,
    counts_hbm,
    new_tables_ref,
    new_acc_ref,
    grad_first_ref,
    grad_second_ref,
    grad_lift_ref,
    grad_press_ref,
    logits_out_ref,
    lift,
    press,
    hidden,
    counts,
    act,
    gl,
    gp,
    gf,
    gsec,
    gt,
    load_sem,
    hidden_sem,
    counts_sem,
):
    n, nt = dims
    me = lax.axis_index("member")
    tpos = lax.axis_index("tower")
    towers, total, hid = hidden.shape
    width, rows = decayed_ref.shape[1:]
    outs = w2h_ref.shape[2]
    rank = lift.shape[1]
    flat = towers * outs
    own = total // n
    chunk = min(256, total)

    loads = []

    def load(source, target):
        loads.append(pltpu.make_async_copy(source, target, load_sem.at[len(loads)]))
        loads[-1].start()

    load(lift_hbm.at[pl.ds(tpos * flat, flat)], lift)
    load(press_hbm.at[pl.ds(tpos * flat, flat)], press)

    def hidden_copy(t, c):
        span = pl.ds(pl.multiple_of(c * chunk, chunk), chunk)
        return pltpu.make_async_copy(
            hidden_hbm.at[t, span], hidden.at[t, span], hidden_sem.at[t, c]
        )

    def counts_copy(t):
        return pltpu.make_async_copy(counts_hbm.at[t], counts.at[t], counts_sem.at[t])

    for t in range(towers):
        for c in range(total // chunk):
            hidden_copy(t, c).start()
        counts_copy(t).start()

    block_hid = hid // n
    window = max(block_hid, 128)
    start = pl.multiple_of((me * block_hid) // 128 * 128, 128)
    gf[...] = jnp.zeros_like(gf)
    gsec[...] = jnp.zeros_like(gsec)
    gl[...] = jnp.zeros_like(gl)
    gp[...] = jnp.zeros_like(gp)
    gt[...] = jnp.zeros_like(gt)
    members_here = chunk // own
    head = head_ref[:, pl.ds(pl.multiple_of(tpos * flat, flat), flat)]
    for copy in loads:
        copy.wait()
    lift_pair = split(lift[...])
    press_pair = split(press[...])

    for t in range(towers):
        counts_copy(t).wait()
        first = split(first_ref[:, t, :])

        @pl.loop(0, total // chunk)
        def _(c):
            hidden_copy(t, c).wait()
            span = pl.ds(pl.multiple_of(c * chunk, chunk), chunk)
            block = gath_ref[pl.ds(c * members_here, members_here)].reshape(chunk, 3 * rank)
            ep = split(block[:, :rank])
            eg = split(block[:, rank : 2 * rank])
            part = slice(t * outs, (t + 1) * outs)
            head_t = head[:, part]
            lift_t = tuple(x[part] for x in lift_pair)
            press_t = tuple(x[part] for x in press_pair)
            w2 = (w2h_ref[t], w2l_ref[t])
            error_all = block[:, 2 * rank : 2 * rank + 1]
            grad_out = head_t * (error_all + dot3(ep, lift_t, NT)) + dot3(eg, press_t, NT)
            h = hidden[t, span, :]
            sig = sigmoid(h)
            a = h * sig
            act[...] = a
            tower_out = tower_out_ref[t, span, :]
            gl[part] += dot3(split((tower_out * head_t).T), ep)
            gp[part] += dot3(split(tower_out.T), eg)
            go = split(grad_out)
            gsec[t] += dot3(split(act[:, pl.ds(start, window)].T), go)
            grad_hidden = split(dot3(go, w2, NT) * (sig * (1.0 + h * (1.0 - sig))))
            pooled = pooled_ref[span, :].T[t * width : (t + 1) * width]
            gf[t] += dot3(split(pooled), grad_hidden)
            grad_pooled = dot3(first, grad_hidden, NT)
            both = dot1(jnp.concatenate(split(grad_pooled), axis=0), counts[t, span, :])
            gt[t] += both[:width] + both[width:]

        shift = pl.multiple_of(me * block_hid - start, min(block_hid, 128))
        grad_second_ref[:, t, :] = gsec[t, pl.ds(shift, block_hid), :]
        grad_first_ref[:, t, :] = gf[t]
        g = gt[t]
        value = acc_ref[t] + jnp.mean(g * g, axis=0, keepdims=True)
        new_acc_ref[t] = value
        new_tables_ref[t] = decayed_ref[t] - LEARN_RATE * g / (jnp.sqrt(value) + EPSILON)

    own_flat = pl.ds(pl.multiple_of(me * (flat // n), flat // n), flat // n)
    grad_lift_ref[...] = gl[own_flat]
    grad_press_ref[...] = gp[own_flat]
    piece = logits_ref.shape[0]
    place = lax.broadcasted_iota(jnp.int32, (piece, piece), 1)
    wanted = lax.broadcasted_iota(jnp.int32, (piece, piece), 0)
    values = jnp.where(place == wanted, logits_ref[:, :1], 0.0)
    logits_out_ref[...] = jnp.sum(values, axis=0, keepdims=True)


def per_device(n, nt, *args):
    bag_ids, touch_ids, elapsed, tables, accumulator, first, second, lift, press, head, labels = args
    towers, _, bags, total = bag_ids.shape
    rows, width = tables.shape[2:]
    fin, _, hid = first.shape
    outs = second.shape[2]
    rank = lift.shape[1]
    flat = towers * outs
    own = total // n
    piece = own // nt
    block_hid = hid // n
    window = max(block_hid, 128)
    vmem = pl.BlockSpec(memory_space=pltpu.VMEM)
    anys = pl.BlockSpec(memory_space=pl.ANY)
    chunk = min(256, total)
    sem = pltpu.SemaphoreType.DMA
    lanes = towers * width
    shape = jax.ShapeDtypeStruct
    logits, decayed, pooled, hidden, gath, counts, w2h, w2l, tower_out = pl.pallas_call(
        functools.partial(gather_kernel, (n, nt)),
        out_shape=(
            shape((piece, rank), F32),
            shape((towers, width, rows), F32),
            shape((total, lanes), F32),
            shape((towers, total, hid), F32),
            shape((n, nt, piece, 3 * rank), F32),
            shape((towers, total, rows), BF16),
            shape((towers, hid, outs), BF16),
            shape((towers, hid, outs), BF16),
            shape((towers, total, outs), F32),
        ),
        in_specs=[vmem] * 4 + [anys] * 4 + [vmem] * 2,
        out_specs=[vmem] * 2 + [anys] * 7,
        scratch_shapes=[
            pltpu.VMEM((towers, fin, hid), BF16),
            pltpu.VMEM((towers, fin, hid), BF16),
            pltpu.VMEM((towers, hid, outs), F32),
            pltpu.VMEM((towers, hid, outs), BF16),
            pltpu.VMEM((towers, hid, outs), BF16),
            pltpu.VMEM((flat, rank), F32),
            pltpu.VMEM((flat, rank), F32),
            pltpu.VMEM((total, 128), F32),
            pltpu.VMEM((towers, total, rows), BF16),
            pltpu.VMEM((n, total, lanes), F32),
            pltpu.VMEM((towers, max(total, fin), hid), F32),
            pltpu.VMEM((towers, total, outs), F32),
            pltpu.VMEM((n, own, lanes), F32),
            sem((n,)),
            sem((n,)),
            pltpu.VMEM((own, 3 * rank), F32),
            pltpu.VMEM((nt, piece, 3 * rank), F32),
            pltpu.VMEM((n, nt, piece, 3 * rank), F32),
            sem((2 * towers + 2,)),
            sem((4 + towers + 1,)),
            sem((towers,)),
            sem((3, n)),
            sem((n,)),
            sem((nt,)),
            sem((nt,)),
            sem((n,)),
            sem((n,)),
            sem((nt,)),
            sem((nt,)),
        ],
        compiler_params=pltpu.CompilerParams(
            collective_id=0, has_side_effects=True, vmem_limit_bytes=67043328
        ),
    )(
        bag_ids[:, 0],
        touch_ids,
        elapsed,
        jnp.transpose(tables[:, 0], (0, 2, 1)),
        first,
        second,
        lift,
        press,
        head[None, :],
        labels,
    )
    out = pl.pallas_call(
        functools.partial(update_kernel, (n, nt)),
        out_shape=(
            shape((towers, width, rows), F32),
            shape((towers, 1, rows), F32),
            shape((width, towers, hid), F32),
            shape((block_hid, towers, outs), F32),
            shape((flat // n, rank), F32),
            shape((flat // n, rank), F32),
            shape((1, piece), F32),
        ),
        grid=(1,),
        in_specs=[vmem] * 4
        + [pl.BlockSpec((width, towers, hid), lambda i: (lax.axis_index("member"), 0, 0))]
        + [vmem] * 4
        + [anys] * 2
        + [vmem]
        + [anys] * 2,
        out_specs=[vmem] * 7,
        scratch_shapes=[
            pltpu.VMEM((flat, rank), F32),
            pltpu.VMEM((flat, rank), F32),
            pltpu.VMEM((towers, total, hid), F32),
            pltpu.VMEM((towers, total, rows), BF16),
            pltpu.VMEM((chunk, hid), F32),
            pltpu.VMEM((flat, rank), F32),
            pltpu.VMEM((flat, rank), F32),
            pltpu.VMEM((towers, width, hid), F32),
            pltpu.VMEM((towers, window, outs), F32),
            pltpu.VMEM((towers, width, rows), F32),
            sem((2,)),
            sem((towers, total // chunk)),
            sem((towers,)),
        ],
        compiler_params=pltpu.CompilerParams(vmem_limit_bytes=67043328),
    )(
        logits,
        tower_out,
        accumulator,
        decayed,
        first,
        pooled,
        gath,
        w2h,
        w2l,
        lift,
        press,
        head[None, :],
        hidden,
        counts,
    )
    new_tables, new_acc, grad_first, grad_second, grad_lift, grad_press, logits = out
    return (
        jnp.transpose(new_tables, (0, 2, 1))[:, None],
        new_acc,
        grad_first,
        grad_second,
        grad_lift,
        grad_press,
        logits,
    )


def solution(mesh):
    placed = (
        P("tower", "member", None, None),
        P("tower", "member", None),
        P("tower", "member", None),
        P("tower", "member", None, None),
        P("tower", "member", None),
        P(None, "tower", None),
        P(None, "tower", None),
        P(),
        P(),
        P(),
        P("member", None),
    )
    return jax.shard_map(
        functools.partial(per_device, mesh.shape["member"], mesh.shape["tower"]),
        mesh=mesh,
        in_specs=placed,
        out_specs=(
            P("tower", "member", None, None),
            P("tower", "member", None),
            P("member", "tower", None),
            P("member", "tower", None),
            P(("tower", "member"), None),
            P(("tower", "member"), None),
            P("member", "tower"),
        ),
        check_vma=False,
    )
```
